32 devices in a mesh: row: 8 (over y, x, core), col: 4 (over z).
Axes of the slice: x: 2, y: 2, z: 4, core: 2. Of those that a mesh axis runs over, the one named last changes fastest.
Arguments:
- pair_rep: bfloat16 [384, 384, 256], P('row', 'col'), may hold values from -6 to 6
- single_rep: bfloat16 [384, 768], replicated, may hold values from -6 to 6
- length: int32 [1], replicated, may hold values from 192 to 384
- pair_gain: float32 [256], replicated, may hold values from 0.25 to 1.75
- pair_proj: bfloat16 [4, 256, 256], replicated, may hold values from -0.375 to 0.375
- bias_weight: bfloat16 [256, 8], replicated, may hold values from -12 to 12
- pair_out_weight: bfloat16 [256, 256], replicated, may hold values from -1 to 1
- single_gain: float32 [768], replicated, may hold values from 0.25 to 1.75
- single_proj: bfloat16 [4, 768, 768], P(None, None, 'col'), may hold values from -0.21875 to 0.21875
- bias_norm_gain: float32 [256], replicated, may hold values from 0.25 to 1.75
- single_bias_weight: bfloat16 [256, 16], replicated, may hold values from -12 to 12
- single_out_weight: bfloat16 [768, 768], P('col'), may hold values from -0.625 to 0.625
Outputs:
- pair_out: bfloat16 [384, 384, 256], P('row', 'col')
- single_out: bfloat16 [384, 768], P('row', 'col')
The draws below stay inside these ranges and needn't reach their ends.
Inputs may be any that keep to these rules, and one draw needn't show every extreme that they name: Positions from length[0] on are padding and never serve as keys.
All inputs are finite; a program needn't handle non-finite values.
Results may differ from the reference program's by a relative error of at most 0.019.
Values may be sent and summed in bfloat16 or wider, within the bound.
A program may use at most 128 MiB of HBM per device.

```python
import math
import jax
import jax.numpy as jnp
from jax import lax

TOKENS = 384
PAIR_DIM = 256
PAIR_HEADS = 8
PAIR_HEAD_DIM = 32
SINGLE_DIM = 768
SINGLE_HEADS = 16
SINGLE_HEAD_DIM = 48


def draw_bias_weight(key, part):
    base = jax.random.normal(jax.random.fold_in(key, 11), (PAIR_DIM, PAIR_HEADS), jnp.float32) / math.sqrt(PAIR_DIM)
    return jnp.clip(base, -12.0, 12.0).astype(jnp.bfloat16)


def draw_single_bias_weight(key, part):
    base = jax.random.normal(jax.random.fold_in(key, 23), (PAIR_DIM, SINGLE_HEADS), jnp.float32) / math.sqrt(PAIR_DIM)
    return jnp.clip(base, -12.0, 12.0).astype(jnp.bfloat16)


def level_of(key, extent, shards, least, top_value):
    gain = 1.0
    for dim, shards_of in shards:
        heights = jax.random.uniform(jax.random.fold_in(jax.random.fold_in(key, 6), dim), (shards_of,), jnp.float32, least / len(shards), top_value / len(shards))
        gain = gain * jnp.repeat(jnp.exp(heights), extent[dim] // shards_of).reshape((-1,) + (1,) * (len(extent) - 1 - dim))
    return gain


def normal_values(own_key, extent, scale, bound, pieces=(), held_as=jnp.bfloat16):
    entries = jax.random.normal(own_key, extent, jnp.float32) * scale
    if len(pieces) > 0:
        entries = level_of(own_key, extent, pieces, -0.22, 0.18) * entries
    return jnp.clip(entries, min=-bound, max=bound).astype(held_as)


def setup_inputs(seed: int = 0) -> dict:
    splits = jax.random.split(jax.random.key(seed), 13)
    return {
        "pair_rep": normal_values(splits[0], (TOKENS, TOKENS, PAIR_DIM), 1.0, 6.0, ((0, 8), (1, 4))),
        "single_rep": normal_values(splits[1], (TOKENS, SINGLE_DIM), 1.0, 6.0),
        "length": jax.random.randint(splits[2], (1,), TOKENS // 2, TOKENS + 1).astype(jnp.int32),
        "pair_gain": jnp.clip(1.0 + 0.15 * jax.random.normal(splits[3], (PAIR_DIM,), jnp.float32), 0.25, 1.75),
        "pair_proj": normal_values(splits[4], (4, PAIR_DIM, PAIR_DIM), PAIR_DIM ** -0.5, 0.375),
        "bias_weight": draw_bias_weight(jax.random.fold_in(splits[12], 71), 0),
        "pair_out_weight": normal_values(splits[6], (PAIR_DIM, PAIR_DIM), (PAIR_DIM // 8) ** -0.5, 1.0),
        "single_gain": jnp.clip(1.0 + 0.15 * jax.random.normal(splits[7], (SINGLE_DIM,), jnp.float32), 0.25, 1.75),
        "single_proj": normal_values(splits[8], (4, SINGLE_DIM, SINGLE_DIM), SINGLE_DIM ** -0.5, 0.21875, ((2, 4),)),
        "bias_norm_gain": jnp.clip(1.0 + 0.15 * jax.random.normal(splits[9], (PAIR_DIM,), jnp.float32), 0.25, 1.75),
        "single_bias_weight": draw_single_bias_weight(jax.random.fold_in(splits[12], 71), 0),
        "single_out_weight": normal_values(splits[11], (SINGLE_DIM, SINGLE_DIM), (SINGLE_DIM // 8) ** -0.5, 0.625, ((0, 4),)),
    }


masked_value = -1e+30

def normalize(values, scales):
    floated = values.astype(jnp.float32)
    center = lax.optimization_barrier(jnp.mean(floated, axis=-1, keepdims=True))
    spread = lax.optimization_barrier(jnp.mean(jnp.square(floated - center), axis=-1, keepdims=True))
    return ((floated - center) * lax.rsqrt(spread + 1e-05) * scales).astype(jnp.bfloat16)

def project(inputs, matrix):
    return jnp.dot(inputs, matrix, preferred_element_type=jnp.float32).astype(jnp.bfloat16)

def softmax_weights(scores):
    row_max = lax.optimization_barrier(jnp.max(scores, axis=-1, keepdims=True))
    exponent = jnp.exp(scores - row_max)
    return (exponent / lax.optimization_barrier(jnp.sum(exponent, axis=-1, keepdims=True))).astype(jnp.bfloat16)

def reference(pair_rep, single_rep, length, pair_gain, pair_proj, bias_weight, pair_out_weight, single_gain, single_proj, bias_norm_gain, single_bias_weight, single_out_weight):
    block_rows = math.gcd(TOKENS, 8)
    groups = TOKENS // block_rows
    stacked = pair_rep.reshape(groups, block_rows, TOKENS, PAIR_DIM)

    def triangle_bias(rows_block):
        normed = normalize(rows_block, pair_gain)
        return project(normed, bias_weight)
    tri_bias = lax.map(triangle_bias, stacked).reshape(TOKENS, TOKENS, PAIR_HEADS)
    tri_bias = jnp.transpose(tri_bias, (2, 0, 1)).astype(jnp.float32)
    usable = jnp.arange(TOKENS, dtype=jnp.int32) < length[0]
    pair_scale = 1.0 / math.sqrt(PAIR_HEAD_DIM)

    def attend(rows_block):
        normed = normalize(rows_block, pair_gain)
        shape_heads = (block_rows, TOKENS, PAIR_HEADS, PAIR_HEAD_DIM)
        queries = project(normed, pair_proj[0]).reshape(shape_heads).astype(jnp.float32)
        key_rows = project(normed, pair_proj[1]).reshape(shape_heads).astype(jnp.float32)
        value_rows = project(normed, pair_proj[2]).reshape(shape_heads).astype(jnp.float32)
        gating = jax.nn.sigmoid(jnp.dot(normed, pair_proj[3], preferred_element_type=jnp.float32))
        scores = jnp.einsum('ijhd,ikhd->ihjk', queries, key_rows) * pair_scale + tri_bias[None]
        scores = jnp.where(usable, scores, masked_value)
        weights = softmax_weights(scores)
        attended = jnp.einsum('ihjk,ikhd->ijhd', weights.astype(jnp.float32), value_rows)
        attended = attended.reshape(block_rows, TOKENS, PAIR_DIM)
        hidden = (gating * attended).astype(jnp.bfloat16)
        updated = (rows_block.astype(jnp.float32) + jnp.dot(hidden, pair_out_weight, preferred_element_type=jnp.float32)).astype(jnp.bfloat16)
        bias_normed = normalize(updated, bias_norm_gain)
        head_bias = project(bias_normed, single_bias_weight)
        return (updated, head_bias)
    pair_out, head_bias = lax.map(attend, stacked)
    pair_out = pair_out.reshape(TOKENS, TOKENS, PAIR_DIM)
    head_bias = jnp.transpose(head_bias.reshape(TOKENS, TOKENS, SINGLE_HEADS), (2, 0, 1)).astype(jnp.float32)
    single_normed = normalize(single_rep, single_gain)
    shape_single = (TOKENS, SINGLE_HEADS, SINGLE_HEAD_DIM)
    s_query = project(single_normed, single_proj[0]).reshape(shape_single).astype(jnp.float32)
    s_key = project(single_normed, single_proj[1]).reshape(shape_single).astype(jnp.float32)
    s_value = project(single_normed, single_proj[2]).reshape(shape_single).astype(jnp.float32)
    s_gate = jax.nn.sigmoid(jnp.dot(single_normed, single_proj[3], preferred_element_type=jnp.float32))
    scores = jnp.einsum('ihd,jhd->hij', s_query, s_key) / math.sqrt(SINGLE_HEAD_DIM) + head_bias
    scores = jnp.where(usable, scores, masked_value)
    weights = softmax_weights(scores)
    blended = jnp.einsum('hij,jhd->ihd', weights.astype(jnp.float32), s_value).reshape(TOKENS, SINGLE_DIM)
    s_hidden = (s_gate * blended).astype(jnp.bfloat16)
    single_out = (single_rep.astype(jnp.float32) + jnp.dot(s_hidden, single_out_weight, preferred_element_type=jnp.float32)).astype(jnp.bfloat16)
    return (pair_out, single_out)
```

```python
import math

import jax
import jax.numpy as jnp
from jax import lax
from jax.experimental import pallas as pl
from jax.experimental.pallas import tpu as pltpu
from jax.sharding import PartitionSpec as P

PAIR_HEADS = 8
PAIR_HEAD_DIM = 32
SINGLE_HEAD_DIM = 48
LOG2E = math.log2(math.e)

masked_value = -1e30
NT = (((1,), (1,)), ((), ()))


def normalize(values, scales):
    floated = values.astype(jnp.float32)
    center = jnp.mean(floated, axis=-1, keepdims=True)
    spread = jnp.mean(jnp.square(floated - center), axis=-1, keepdims=True)
    return ((floated - center) * lax.rsqrt(spread + 1e-05) * scales).astype(jnp.bfloat16)


def project(inputs, matrix):
    return jnp.dot(inputs, matrix, preferred_element_type=jnp.float32).astype(jnp.bfloat16)


def row_update(rep, gain, proj_ref, out_weight, bias_of):
    channels = rep.shape[1]
    half = channels // 2
    heads_per_half = PAIR_HEADS // 2
    normed = normalize(rep, gain)
    f32 = jnp.float32
    query = jnp.dot(normed, proj_ref[0], preferred_element_type=f32)
    query = (query * (LOG2E / math.sqrt(PAIR_HEAD_DIM))).astype(jnp.bfloat16)
    key = project(normed, proj_ref[1])
    value = project(normed, proj_ref[2])
    gate = jax.nn.sigmoid(jnp.dot(normed, proj_ref[3], preferred_element_type=f32))
    head_of_lane = lax.broadcasted_iota(jnp.int32, (1, half), 1) // PAIR_HEAD_DIM
    halves = []
    for side in range(2):
        span = slice(side * half, (side + 1) * half)
        q_half, k_half, v_half = query[:, span], key[:, span], value[:, span]
        top = bottom = None
        for sub in range(heads_per_half):
            head = side * heads_per_half + sub
            mine = head_of_lane == sub
            q_head = jnp.where(mine, q_half, jnp.zeros_like(q_half))
            scores = lax.dot_general(q_head, k_half, NT, preferred_element_type=f32)
            scores = scores + bias_of(head)
            peak = jnp.max(scores, axis=-1, keepdims=True)
            exponent = jnp.exp2(scores - peak).astype(jnp.bfloat16)
            v_ext = jnp.concatenate([v_half, jnp.ones_like(v_half)], axis=1)
            both = jnp.dot(exponent, v_ext, preferred_element_type=f32)
            num, den = both[:, :half], both[:, half:]
            top = num if top is None else jnp.where(mine, num, top)
            bottom = den if bottom is None else jnp.where(mine, den, bottom)
        halves.append(top / bottom)
    attended = jnp.concatenate(halves, axis=1)
    hidden = (gate * attended).astype(jnp.bfloat16)
    return (
        rep.astype(f32) + jnp.dot(hidden, out_weight, preferred_element_type=f32)
    ).astype(jnp.bfloat16)


def slab_kernel(
    length_ref, rep_ref, bias_ref, gain_ref, proj_ref, out_weight_ref, bias_gain_ref, head_weight_ref,
    new_ref, head_bias_ref, bias_held,
):
    bands, heads, band_rows, tokens = bias_ref.shape

    @pl.when(pl.program_id(0) == 0)
    def _():
        usable = lax.broadcasted_iota(jnp.int32, (1, 1, tokens), 2) < length_ref[0]
        for band in range(bands):
            piece = bias_ref[band].astype(jnp.float32) * LOG2E
            bias_held[:, band * band_rows : (band + 1) * band_rows, :] = jnp.where(
                usable, piece, masked_value
            )

    updated = row_update(
        rep_ref[0], gain_ref[...], proj_ref, out_weight_ref[...], lambda head: bias_held[head]
    )
    new_ref[0] = updated
    again = normalize(updated, bias_gain_ref[...])
    head_bias_ref[0] = lax.dot_general(
        head_weight_ref[...], again, NT, preferred_element_type=jnp.float32
    ).astype(jnp.bfloat16)


def slab_attention(length, slab, bias, gain, proj, out_weight, bias_gain, head_weight_t):
    rows, tokens, channels = slab.shape
    single_heads = head_weight_t.shape[0]
    whole = lambda shape: pl.BlockSpec(
        shape, lambda i: (0,) * len(shape), pipeline_mode=pl.Buffered(1)
    )
    return pl.pallas_call(
        slab_kernel,
        grid=(rows,),
        in_specs=[
            pl.BlockSpec(memory_space=pltpu.SMEM),
            pl.BlockSpec((1, tokens, channels), lambda i: (i, 0, 0)),
            whole(bias.shape),
            whole((1, channels)),
            whole(proj.shape),
            whole(out_weight.shape),
            whole((1, channels)),
            whole(head_weight_t.shape),
        ],
        out_specs=[
            pl.BlockSpec((1, tokens, channels), lambda i: (i, 0, 0)),
            pl.BlockSpec((1, single_heads, tokens), lambda i: (i, 0, 0)),
        ],
        out_shape=[
            jax.ShapeDtypeStruct(slab.shape, jnp.bfloat16),
            jax.ShapeDtypeStruct((rows, single_heads, tokens), jnp.bfloat16),
        ],
        scratch_shapes=[pltpu.VMEM((PAIR_HEADS, tokens, tokens), jnp.float32)],
        compiler_params=pltpu.CompilerParams(vmem_limit_bytes=60 * 2**20),
        name="slab_attention",
    )(length, slab, bias, gain, proj, out_weight, bias_gain, head_weight_t)


def per_device(
    pair_rep,
    single_rep,
    length,
    pair_gain,
    pair_proj,
    bias_weight,
    pair_out_weight,
    single_gain,
    single_proj,
    bias_norm_gain,
    single_bias_weight,
    single_out_weight,
):
    rows_here, cols_here, channels = pair_rep.shape
    tokens = rows_here * lax.axis_size("row")
    valid_length = length[0]
    normed = normalize(pair_rep, pair_gain)
    local_bias = jnp.einsum(
        "rcd,dh->hrc", normed, bias_weight, preferred_element_type=jnp.float32
    ).astype(jnp.bfloat16)
    row_band = lax.all_gather(local_bias, "col", axis=2, tiled=True)
    bias_bands = lax.all_gather(row_band, "row")
    row_slab = lax.all_to_all(pair_rep, "col", split_axis=0, concat_axis=1, tiled=True)
    updated_slab, slab_head_bias = slab_attention(
        length,
        row_slab,
        bias_bands,
        pair_gain[None],
        pair_proj,
        pair_out_weight,
        bias_norm_gain[None],
        single_bias_weight.T,
    )
    pair_out = lax.all_to_all(updated_slab, "col", split_axis=1, concat_axis=0, tiled=True)
    head_bias = lax.all_to_all(slab_head_bias, "col", split_axis=1, concat_axis=0, tiled=True)
    head_bias = jnp.transpose(head_bias, (1, 0, 2))
    single_normed = normalize(single_rep, single_gain)
    row_start = lax.axis_index("row") * rows_here
    mine = lax.dynamic_slice_in_dim(single_normed, row_start, rows_here, 0)
    local_width = single_proj.shape[2]
    heads_here = local_width // SINGLE_HEAD_DIM
    s_query = project(mine, single_proj[0]).reshape(rows_here, heads_here, SINGLE_HEAD_DIM)
    s_key = project(single_normed, single_proj[1]).reshape(tokens, heads_here, SINGLE_HEAD_DIM)
    s_value = project(single_normed, single_proj[2]).reshape(tokens, heads_here, SINGLE_HEAD_DIM)
    s_gate = jax.nn.sigmoid(jnp.dot(mine, single_proj[3], preferred_element_type=jnp.float32))
    scores = jnp.einsum(
        "ihd,jhd->hij", s_query, s_key, preferred_element_type=jnp.float32
    ) / math.sqrt(SINGLE_HEAD_DIM)
    scores = scores + head_bias.astype(jnp.float32)
    token_usable = jnp.arange(tokens, dtype=jnp.int32) < valid_length
    scores = jnp.where(token_usable, scores, masked_value)
    row_max = jnp.max(scores, axis=-1, keepdims=True)
    exponent = jnp.exp(scores - row_max)
    weights = (exponent / jnp.sum(exponent, axis=-1, keepdims=True)).astype(jnp.bfloat16)
    blended = jnp.einsum(
        "hij,jhd->ihd", weights, s_value, preferred_element_type=jnp.float32
    ).reshape(rows_here, local_width)
    s_hidden = (s_gate * blended).astype(jnp.bfloat16)
    partial_value = jnp.dot(s_hidden, single_out_weight, preferred_element_type=jnp.float32)
    reduced = lax.psum_scatter(
        partial_value.astype(jnp.bfloat16), "col", scatter_dimension=1, tiled=True
    ).astype(jnp.float32)
    col_start = lax.axis_index("col") * local_width
    residual = lax.dynamic_slice(single_rep, (row_start, col_start), (rows_here, local_width))
    single_out = (residual.astype(jnp.float32) + reduced).astype(jnp.bfloat16)
    return (pair_out, single_out)


def solution(mesh):
    in_specs = (
        P("row", "col", None),
        P(),
        P(),
        P(),
        P(),
        P(),
        P(),
        P(),
        P(None, None, "col"),
        P(),
        P(),
        P("col", None),
    )
    out_specs = (P("row", "col", None), P("row", "col"))
    return jax.shard_map(
        per_device, mesh=mesh, in_specs=in_specs, out_specs=out_specs, check_vma=False
    )
```

```python
import math

import jax
import jax.numpy as jnp
from jax import lax
from jax.experimental import pallas as pl
from jax.experimental.pallas import tpu as pltpu
from jax.sharding import PartitionSpec as P

PAIR_HEADS = 8
PAIR_HEAD_DIM = 32
SINGLE_HEAD_DIM = 48
LOG2E = math.log2(math.e)

masked_value = -1e30
NT = (((1,), (1,)), ((), ()))


def normalize(values, scales):
    floated = values.astype(jnp.float32)
    center = jnp.mean(floated, axis=-1, keepdims=True)
    spread = jnp.mean(jnp.square(floated - center), axis=-1, keepdims=True)
    return ((floated - center) * lax.rsqrt(spread + 1e-05) * scales).astype(jnp.bfloat16)


def project(inputs, matrix):
    return jnp.dot(inputs, matrix, preferred_element_type=jnp.float32).astype(jnp.bfloat16)


def row_update(rep, gain, proj_ref, out_weight, bias_of):
    channels = rep.shape[1]
    half = channels // 2
    heads_per_half = PAIR_HEADS // 2
    normed = normalize(rep, gain)
    f32 = jnp.float32
    query = jnp.dot(normed, proj_ref[0], preferred_element_type=f32)
    query = (query * (LOG2E / math.sqrt(PAIR_HEAD_DIM))).astype(jnp.bfloat16)
    key = project(normed, proj_ref[1])
    value = project(normed, proj_ref[2])
    gate = jax.nn.sigmoid(jnp.dot(normed, proj_ref[3], preferred_element_type=f32))
    head_of_lane = lax.broadcasted_iota(jnp.int32, (1, half), 1) // PAIR_HEAD_DIM
    halves = []
    for side in range(2):
        span = slice(side * half, (side + 1) * half)
        q_half, k_half, v_half = query[:, span], key[:, span], value[:, span]
        top = bottom = None
        for sub in range(heads_per_half):
            head = side * heads_per_half + sub
            mine = head_of_lane == sub
            q_head = jnp.where(mine, q_half, jnp.zeros_like(q_half))
            scores = lax.dot_general(q_head, k_half, NT, preferred_element_type=f32)
            scores = scores + bias_of(head)
            peak = jnp.max(scores, axis=-1, keepdims=True)
            exponent = jnp.exp2(scores - peak).astype(jnp.bfloat16)
            v_ext = jnp.concatenate([v_half, jnp.ones_like(v_half)], axis=1)
            both = jnp.dot(exponent, v_ext, preferred_element_type=f32)
            num, den = both[:, :half], both[:, half:]
            top = num if top is None else jnp.where(mine, num, top)
            bottom = den if bottom is None else jnp.where(mine, den, bottom)
        halves.append(top / bottom)
    attended = jnp.concatenate(halves, axis=1)
    hidden = (gate * attended).astype(jnp.bfloat16)
    return (
        rep.astype(f32) + jnp.dot(hidden, out_weight, preferred_element_type=f32)
    ).astype(jnp.bfloat16)


def slot(ref, *index):
    return ref.at[index]


def window_kernel(
    length_ref, pair_ref, tri_ref, single_ref, rest_ref, gain_ref, proj_ref, out_weight_ref,
    bias_gain_ref, head_weight_ref, single_gain_ref, single_proj_ref, single_out_ref,
    pair_out_ref, single_new_ref,
    slab, fresh, bands, bias_held, head_kept, head_sent, head_got, head_full,
    s_query, s_key, s_value, s_gate, part_sent, part_got,
    in_send, in_recv, in_own, out_send, out_recv, out_own,
    col_send, col_recv, col_own, chip_send, chip_recv, core_send, core_recv,
    head_send, head_recv, part_send, part_recv,
):
    f32 = jnp.float32
    slab_rows, cols, cols_here, channels = slab.shape
    rows, _, heads, rows_here, _ = bands.shape
    tokens = cols * cols_here
    chips = rows // 2
    row, col = lax.axis_index("row"), lax.axis_index("col")
    chip, core = row // 2, lax.rem(row, 2)
    partner = chip * 2 + 1 - core
    mesh_id = pl.DeviceIdType.MESH

    def peer(step):
        return lax.rem(col + step, cols)

    def chip_row(step):
        return lax.rem(chip + step, chips) * 2 + core

    def chip_back(step):
        return lax.rem(chip + chips - step, chips) * 2 + core

    barrier = pltpu.get_barrier_semaphore()
    for step in range(1, cols):
        pl.semaphore_signal(barrier, inc=1, device_id=(row, peer(step)), device_id_type=mesh_id)
    for step in range(1, chips):
        pl.semaphore_signal(barrier, inc=1, device_id=(chip_row(step), col), device_id_type=mesh_id)
    pl.semaphore_signal(barrier, inc=1, device_id=(partner, col), device_id_type=mesh_id)
    pl.semaphore_wait(barrier, cols + chips - 1)

    def remote(src, dst, send, recv, to):
        return pltpu.make_async_remote_copy(
            src_ref=src, dst_ref=dst, send_sem=send, recv_sem=recv,
            device_id=to, device_id_type=mesh_id,
        )

    def col_copy(step):
        return remote(
            tri_ref, slot(bands, row, col), col_send.at[step], col_recv.at[step], (row, peer(step))
        )

    def chip_copy(step):
        return remote(
            slot(bands, row), slot(bands, row), chip_send.at[step], chip_recv.at[step],
            (chip_row(step), col),
        )

    def core_copy(step):
        band = chip_back(step)
        return remote(
            slot(bands, band), slot(bands, band), core_send.at[step], core_recv.at[step],
            (partner, col),
        )

    def in_copy(s, step):
        to = peer(step)
        return remote(
            slot(pair_ref, to * slab_rows + s), slot(slab, s, col),
            in_send.at[s, step], in_recv.at[s, step], (row, to),
        )

    def own_in(s):
        return pltpu.make_async_copy(
            slot(pair_ref, col * slab_rows + s), slot(slab, s, col), in_own.at[s]
        )

    def out_copy(s, step):
        to = peer(step)
        return remote(
            slot(fresh, s, to), slot(pair_out_ref, col * slab_rows + s),
            out_send.at[s, step], out_recv.at[s, step], (row, to),
        )

    def own_out(s):
        return pltpu.make_async_copy(
            slot(fresh, s, col), slot(pair_out_ref, col * slab_rows + s), out_own.at[s]
        )

    def head_copy(step):
        to = peer(step)
        return remote(
            slot(head_sent, to), slot(head_got, col), head_send.at[step], head_recv.at[step],
            (row, to),
        )

    def part_copy(step):
        to = peer(step)
        return remote(
            slot(part_sent, to), slot(part_got, step), part_send.at[step], part_recv.at[step],
            (row, to),
        )

    for step in range(1, cols):
        col_copy(step).start()
    own_block = pltpu.make_async_copy(tri_ref, slot(bands, row, col), col_own)
    own_block.start()

    @pl.loop(0, slab_rows)
    def _(s):
        own_in(s).start()
        for step in range(1, cols):
            in_copy(s, step).start()

    for step in range(1, cols):
        col_copy(step).wait_recv()
    own_block.wait()
    for step in range(1, chips):
        chip_copy(step).start()
    core_copy(0).start()

    s_normed = normalize(single_ref[...], single_gain_ref[...])
    s_key[...] = project(s_normed, single_proj_ref[1])
    s_value[...] = project(s_normed, single_proj_ref[2])
    mine = normalize(
        single_ref[pl.ds(pl.multiple_of(row * rows_here, rows_here), rows_here), :],
        single_gain_ref[...],
    )
    s_query[...] = (
        jnp.dot(mine, single_proj_ref[0], preferred_element_type=f32)
        * (LOG2E / math.sqrt(SINGLE_HEAD_DIM))
    ).astype(jnp.bfloat16)
    s_gate[...] = jax.nn.sigmoid(jnp.dot(mine, single_proj_ref[3], preferred_element_type=f32))

    def take_band(band):
        start = pl.multiple_of(band * rows_here, rows_here)
        for part in range(cols):
            usable = (
                lax.broadcasted_iota(jnp.int32, (1, 1, cols_here), 2) + part * cols_here
                < length_ref[0]
            )
            piece = bands[band, part].astype(f32) * LOG2E
            bias_held[:, pl.ds(start, rows_here), part * cols_here : (part + 1) * cols_here] = (
                jnp.where(usable, piece, masked_value)
            )

    take_band(row)
    for step in range(1, chips):
        chip_copy(step).wait_recv()
        core_copy(step).start()
        take_band(chip_back(step))
    for step in range(chips):
        core_copy(step).wait_recv()
        take_band(chip_back(step) + 1 - 2 * core)

    early = slab_rows // 2

    def one_row(s):
        own_in(s).wait()
        for step in range(1, cols):
            in_copy(s, step).wait_recv()
        rep = slab[s].reshape(tokens, channels)
        updated = row_update(
            rep, gain_ref[...], proj_ref, out_weight_ref[...], lambda head: bias_held[head]
        )
        fresh[s] = updated.reshape(cols, cols_here, channels)
        again = normalize(updated, bias_gain_ref[...])
        head_kept[:, s, :] = lax.dot_general(
            head_weight_ref[...], again, NT, preferred_element_type=f32
        )

    def send_row(s):
        own_out(s).start()
        for step in range(1, cols):
            out_copy(s, step).start()

    @pl.loop(0, slab_rows)
    def _(s):
        one_row(s)

        @pl.when(s < early)
        def _():
            send_row(s)

    head_sent[...] = head_kept[...].astype(jnp.bfloat16).reshape(head_sent.shape)
    for step in range(1, cols):
        head_copy(step).start()

    @pl.loop(early, slab_rows)
    def _(s):
        send_row(s)

    for step in range(1, cols):
        head_copy(step).wait_recv()
    for part in range(cols):
        span = slice(part * slab_rows, (part + 1) * slab_rows)

        @pl.when(col == part)
        def _():
            head_full[:, span, :] = head_sent[part].astype(f32) * LOG2E

        @pl.when(col != part)
        def _():
            head_full[:, span, :] = head_got[part].astype(f32) * LOG2E

    width = s_key.shape[1]
    s_heads = head_full.shape[0]
    usable = lax.broadcasted_iota(jnp.int32, (1, tokens), 1) < length_ref[0]
    head_of_lane = lax.broadcasted_iota(jnp.int32, (1, width), 1) // SINGLE_HEAD_DIM
    blended = jnp.zeros((rows_here, width), f32)
    for head in range(s_heads):
        here = head_of_lane == head
        q_head = jnp.where(here, s_query[...], jnp.zeros_like(s_query[...]))
        scores = lax.dot_general(q_head, s_key[...], NT, preferred_element_type=f32)
        scores = jnp.where(usable, scores + head_full[head], masked_value)
        exponent = jnp.exp2(scores - jnp.max(scores, axis=-1, keepdims=True))
        total = jnp.sum(exponent, axis=-1, keepdims=True)
        weights = (exponent / total).astype(jnp.bfloat16)
        blended = jnp.where(
            here, jnp.dot(weights, s_value[...], preferred_element_type=f32), blended
        )
    s_hidden = (s_gate[...] * blended).astype(jnp.bfloat16)
    for part in range(cols):
        share = jnp.dot(s_hidden, single_out_ref[part], preferred_element_type=f32)
        part_sent[part] = share.astype(jnp.bfloat16)
    for step in range(1, cols):
        part_copy(step).start()
    total = rest_ref[...].astype(f32) + part_sent[col].astype(f32)
    for step in range(1, cols):
        part_copy(step).wait_recv()
        total = total + part_got[step].astype(f32)
    single_new_ref[...] = total.astype(jnp.bfloat16)

    for step in range(1, cols):
        col_copy(step).wait_send()
        head_copy(step).wait_send()
        part_copy(step).wait_send()
    for step in range(1, chips):
        chip_copy(step).wait_send()
    for step in range(chips):
        core_copy(step).wait_send()

    @pl.loop(0, slab_rows)
    def _(s):
        own_out(s).wait()
        for step in range(1, cols):
            in_copy(s, step).wait_send()
            out_copy(s, step).wait_send()
            out_copy(s, step).wait_recv()


def per_device(
    pair_rep,
    single_rep,
    length,
    pair_gain,
    pair_proj,
    bias_weight,
    pair_out_weight,
    single_gain,
    single_proj,
    bias_norm_gain,
    single_bias_weight,
    single_out_weight,
):
    rows_here, cols_here, channels = pair_rep.shape
    rows, cols = lax.axis_size("row"), lax.axis_size("col")
    tokens = rows_here * rows
    slab_rows = rows_here // cols
    chips = rows // 2
    heads = bias_weight.shape[1]
    single_heads = single_bias_weight.shape[1]
    heads_here = single_heads // cols
    width = single_proj.shape[2]
    normed = normalize(pair_rep, pair_gain)
    local_bias = jnp.einsum(
        "rcd,dh->hrc", normed, bias_weight, preferred_element_type=jnp.float32
    ).astype(jnp.bfloat16)
    row_start = lax.axis_index("row") * rows_here
    col_start = lax.axis_index("col") * width
    residual = lax.dynamic_slice(single_rep, (row_start, col_start), (rows_here, width))
    out_pieces = single_out_weight.reshape(width, cols, width).transpose(1, 0, 2)
    bf16, f32 = jnp.bfloat16, jnp.float32
    dma = pltpu.SemaphoreType.DMA
    anywhere = pl.BlockSpec(memory_space=pl.ANY)
    held = pl.BlockSpec(memory_space=pltpu.VMEM)
    pair_out, single_out = pl.pallas_call(
        window_kernel,
        in_specs=[pl.BlockSpec(memory_space=pltpu.SMEM), anywhere] + [held] * 11,
        out_specs=[anywhere, held],
        out_shape=[
            jax.ShapeDtypeStruct(pair_rep.shape, bf16),
            jax.ShapeDtypeStruct((rows_here, width), bf16),
        ],
        scratch_shapes=[
            pltpu.VMEM((slab_rows, cols, cols_here, channels), bf16),
            pltpu.VMEM((slab_rows, cols, cols_here, channels), bf16),
            pltpu.VMEM((rows, cols, heads, rows_here, cols_here), bf16),
            pltpu.VMEM((heads, tokens, tokens), f32),
            pltpu.VMEM((single_heads, slab_rows, tokens), f32),
            pltpu.VMEM((cols, heads_here, slab_rows, tokens), bf16),
            pltpu.VMEM((cols, heads_here, slab_rows, tokens), bf16),
            pltpu.VMEM((heads_here, rows_here, tokens), f32),
            pltpu.VMEM((rows_here, width), bf16),
            pltpu.VMEM((tokens, width), bf16),
            pltpu.VMEM((tokens, width), bf16),
            pltpu.VMEM((rows_here, width), f32),
            pltpu.VMEM((cols, rows_here, width), bf16),
            pltpu.VMEM((cols, rows_here, width), bf16),
            dma((slab_rows, cols)),
            dma((slab_rows, cols)),
            dma((slab_rows,)),
            dma((slab_rows, cols)),
            dma((slab_rows, cols)),
            dma((slab_rows,)),
            dma((cols,)),
            dma((cols,)),
            dma,
            dma((chips,)),
            dma((chips,)),
            dma((chips,)),
            dma((chips,)),
            dma((cols,)),
            dma((cols,)),
            dma((cols,)),
            dma((cols,)),
        ],
        compiler_params=pltpu.CompilerParams(
            collective_id=0, has_side_effects=True, vmem_limit_bytes=60 * 2**20
        ),
        name="window",
    )(
        length, pair_rep, local_bias, single_rep, residual, pair_gain[None], pair_proj,
        pair_out_weight, bias_norm_gain[None], single_bias_weight.T, single_gain[None],
        single_proj, out_pieces,
    )
    return (pair_out, single_out)


def solution(mesh):
    in_specs = (
        P("row", "col", None),
        P(),
        P(),
        P(),
        P(),
        P(),
        P(),
        P(),
        P(None, None, "col"),
        P(),
        P(),
        P("col", None),
    )
    out_specs = (P("row", "col", None), P("row", "col"))
    return jax.shard_map(
        per_device, mesh=mesh, in_specs=in_specs, out_specs=out_specs, check_vma=False
    )
```

```python
import math

import jax
import jax.numpy as jnp
from jax import lax
from jax.experimental import pallas as pl
from jax.experimental.pallas import tpu as pltpu
from jax.sharding import PartitionSpec as P

PAIR_HEADS = 8
PAIR_HEAD_DIM = 32
SINGLE_HEAD_DIM = 48
LOG2E = math.log2(math.e)

masked_value = -1e30
NT = (((1,), (1,)), ((), ()))


def normalize(values, scales):
    floated = values.astype(jnp.float32)
    center = jnp.mean(floated, axis=-1, keepdims=True)
    spread = jnp.mean(jnp.square(floated - center), axis=-1, keepdims=True)
    return ((floated - center) * lax.rsqrt(spread + 1e-05) * scales).astype(jnp.bfloat16)


def project(inputs, matrix):
    return jnp.dot(inputs, matrix, preferred_element_type=jnp.float32).astype(jnp.bfloat16)


def project_t(inputs, matrix):
    return lax.dot_general(inputs, matrix, NT, preferred_element_type=jnp.float32).astype(
        jnp.bfloat16
    )


def row_update(rep, gain, proj_ref, out_weight, bias_of):
    channels = rep.shape[1]
    half = channels // 2
    heads_per_half = PAIR_HEADS // 2
    normed = normalize(rep, gain)
    f32 = jnp.float32
    query = jnp.dot(normed, proj_ref[0], preferred_element_type=f32)
    query = (query * (LOG2E / math.sqrt(PAIR_HEAD_DIM))).astype(jnp.bfloat16)
    key = project(normed, proj_ref[1])
    value = project(normed, proj_ref[2])
    gate = jax.nn.sigmoid(jnp.dot(normed, proj_ref[3], preferred_element_type=f32))
    head_of_lane = lax.broadcasted_iota(jnp.int32, (1, half), 1) // PAIR_HEAD_DIM
    halves = []
    for side in range(2):
        span = slice(side * half, (side + 1) * half)
        q_half, k_half, v_half = query[:, span], key[:, span], value[:, span]
        top = bottom = None
        for sub in range(heads_per_half):
            head = side * heads_per_half + sub
            mine = head_of_lane == sub
            q_head = jnp.where(mine, q_half, jnp.zeros_like(q_half))
            scores = lax.dot_general(q_head, k_half, NT, preferred_element_type=f32)
            scores = scores + bias_of(head)
            peak = jnp.max(scores, axis=-1, keepdims=True)
            exponent = jnp.exp2(scores - peak).astype(jnp.bfloat16)
            v_ext = jnp.concatenate([v_half, jnp.ones_like(v_half)], axis=1)
            both = jnp.dot(exponent, v_ext, preferred_element_type=f32)
            num, den = both[:, :half], both[:, half:]
            top = num if top is None else jnp.where(mine, num, top)
            bottom = den if bottom is None else jnp.where(mine, den, bottom)
        halves.append(top / bottom)
    attended = jnp.concatenate(halves, axis=1)
    hidden = (gate * attended).astype(jnp.bfloat16)
    return (
        rep.astype(f32) + jnp.dot(hidden, out_weight, preferred_element_type=f32)
    ).astype(jnp.bfloat16)


def slot(ref, *index):
    return ref.at[index]


def window_kernel(
    length_ref, pair_ref, single_hbm, proj_hbm, out_weight_hbm, single_proj_hbm, single_out_hbm,
    gain_ref, tri_weight_ref, bias_gain_ref, head_weight_ref, single_gain_ref,
    pair_out_ref, single_new_ref,
    local, tri_kept, tri_ref, single_ref, proj_ref, out_weight_ref, single_proj_ref, single_out_ref,
    rest_ref, local_sem, weight_sem,
    slab, fresh, bands, bias_held, head_kept, head_sent, head_got, head_full,
    s_query, s_key, s_value, s_gate, part_sent, part_got,
    in_send, in_recv, in_own, out_send, out_recv, out_own,
    col_send, col_recv, col_own, chip_send, chip_recv, core_send, core_recv,
    head_send, head_recv, part_send, part_recv,
):
    f32 = jnp.float32
    slab_rows, cols, cols_here, channels = slab.shape
    rows, _, heads, rows_here, _ = bands.shape
    tokens = cols * cols_here
    chips = rows // 2
    row, col = lax.axis_index("row"), lax.axis_index("col")
    chip, core = row // 2, lax.rem(row, 2)
    partner = chip * 2 + 1 - core
    mesh_id = pl.DeviceIdType.MESH

    def peer(step):
        return lax.rem(col + step, cols)

    def chip_row(step):
        return lax.rem(chip + step, chips) * 2 + core

    def chip_back(step):
        return lax.rem(chip + chips - step, chips) * 2 + core

    def local_copy(part):
        span = pl.ds(part * slab_rows, slab_rows)
        return pltpu.make_async_copy(pair_ref.at[span], local.at[span], local_sem.at[part])

    weight_copies = [
        pltpu.make_async_copy(src, dst, weight_sem.at[i])
        for i, (src, dst) in enumerate(
            (
                (single_hbm, single_ref),
                (single_proj_hbm, single_proj_ref),
                (proj_hbm, proj_ref),
                (out_weight_hbm, out_weight_ref),
                (single_out_hbm, single_out_ref),
            )
        )
    ]
    for part in range(cols):
        local_copy(part).start()
    for copy in weight_copies:
        copy.start()

    barrier = pltpu.get_barrier_semaphore()
    for step in range(1, cols):
        pl.semaphore_signal(barrier, inc=1, device_id=(row, peer(step)), device_id_type=mesh_id)
    for step in range(1, chips):
        pl.semaphore_signal(barrier, inc=1, device_id=(chip_row(step), col), device_id_type=mesh_id)
    pl.semaphore_signal(barrier, inc=1, device_id=(partner, col), device_id_type=mesh_id)
    pl.semaphore_wait(barrier, cols + chips - 1)

    def remote(src, dst, send, recv, to):
        return pltpu.make_async_remote_copy(
            src_ref=src, dst_ref=dst, send_sem=send, recv_sem=recv,
            device_id=to, device_id_type=mesh_id,
        )

    def col_copy(step):
        return remote(
            tri_ref, slot(bands, row, col), col_send.at[step], col_recv.at[step], (row, peer(step))
        )

    def chip_copy(step):
        return remote(
            slot(bands, row), slot(bands, row), chip_send.at[step], chip_recv.at[step],
            (chip_row(step), col),
        )

    def core_copy(step):
        band = chip_back(step)
        return remote(
            slot(bands, band), slot(bands, band), core_send.at[step], core_recv.at[step],
            (partner, col),
        )

    def in_copy(s, step):
        to = peer(step)
        return remote(
            slot(pair_ref, to * slab_rows + s), slot(slab, s, col),
            in_send.at[s, step], in_recv.at[s, step], (row, to),
        )

    def own_in(s):
        return pltpu.make_async_copy(
            slot(pair_ref, col * slab_rows + s), slot(slab, s, col), in_own.at[s]
        )

    def out_copy(s, step):
        to = peer(step)
        return remote(
            slot(fresh, s, to), slot(pair_out_ref, col * slab_rows + s),
            out_send.at[s, step], out_recv.at[s, step], (row, to),
        )

    def own_out(s):
        return pltpu.make_async_copy(
            slot(fresh, s, col), slot(pair_out_ref, col * slab_rows + s), out_own.at[s]
        )

    def head_copy(step):
        to = peer(step)
        return remote(
            slot(head_sent, to), slot(head_got, col), head_send.at[step], head_recv.at[step],
            (row, to),
        )

    def part_copy(step):
        to = peer(step)
        return remote(
            slot(part_sent, to), slot(part_got, step), part_send.at[step], part_recv.at[step],
            (row, to),
        )

    def bring_row(s):
        own_in(s).start()
        for step in range(1, cols):
            in_copy(s, step).start()

    bring_row(0)
    group = math.gcd(slab_rows, 6)
    for part in range(cols):
        local_copy(part).wait()

        @pl.loop(0, slab_rows // group)
        def _(i):
            for j in range(group):
                r = part * slab_rows + i * group + j
                tri_kept[:, r, :] = lax.dot_general(
                    tri_weight_ref[...], normalize(local[r], gain_ref[...]), NT,
                    preferred_element_type=f32,
                )

    tri_ref[...] = tri_kept[...].astype(jnp.bfloat16)
    for step in range(1, cols):
        col_copy(step).start()
    own_block = pltpu.make_async_copy(tri_ref, slot(bands, row, col), col_own)
    own_block.start()

    @pl.loop(1, slab_rows)
    def _(s):
        bring_row(s)

    for copy in weight_copies:
        copy.wait()

    for step in range(1, cols):
        col_copy(step).wait_recv()
    own_block.wait()
    for step in range(1, chips):
        chip_copy(step).start()
    core_copy(0).start()

    s_normed = normalize(single_ref[...], single_gain_ref[...])
    s_key[...] = project_t(s_normed, single_proj_ref[1])
    s_value[...] = project_t(s_normed, single_proj_ref[2])
    width = s_key.shape[1]
    my_rows = pl.ds(pl.multiple_of(row * rows_here, rows_here), rows_here)
    for part in range(cols):

        @pl.when(col == part)
        def _():
            rest_ref[...] = single_ref[my_rows, part * width : (part + 1) * width]

    mine = normalize(
        single_ref[my_rows, :],
        single_gain_ref[...],
    )
    s_query[...] = (
        lax.dot_general(mine, single_proj_ref[0], NT, preferred_element_type=f32)
        * (LOG2E / math.sqrt(SINGLE_HEAD_DIM))
    ).astype(jnp.bfloat16)
    s_gate[...] = jax.nn.sigmoid(
        lax.dot_general(mine, single_proj_ref[3], NT, preferred_element_type=f32)
    )

    def take_band(band):
        start = pl.multiple_of(band * rows_here, rows_here)
        for part in range(cols):
            usable = (
                lax.broadcasted_iota(jnp.int32, (1, 1, cols_here), 2) + part * cols_here
                < length_ref[0]
            )
            piece = bands[band, part].astype(f32) * LOG2E
            bias_held[:, pl.ds(start, rows_here), part * cols_here : (part + 1) * cols_here] = (
                jnp.where(usable, piece, masked_value)
            )

    take_band(row)
    for step in range(1, chips):
        chip_copy(step).wait_recv()
        core_copy(step).start()
        take_band(chip_back(step))
    for step in range(chips):
        core_copy(step).wait_recv()
        take_band(chip_back(step) + 1 - 2 * core)

    early = 2 * slab_rows // 3
    late = slab_rows - slab_rows // 6

    def one_row(s):
        own_in(s).wait()
        for step in range(1, cols):
            in_copy(s, step).wait_recv()
        rep = slab[s].reshape(tokens, channels)
        updated = row_update(
            rep, gain_ref[...], proj_ref, out_weight_ref[...], lambda head: bias_held[head]
        )
        fresh[s] = updated.reshape(cols, cols_here, channels)
        again = normalize(updated, bias_gain_ref[...])
        head_kept[:, s, :] = lax.dot_general(
            head_weight_ref[...], again, NT, preferred_element_type=f32
        )

    def send_row(s):
        own_out(s).start()
        for step in range(1, cols):
            out_copy(s, step).start()

    @pl.loop(0, slab_rows)
    def _(s):
        one_row(s)

        @pl.when(s < early)
        def _():
            send_row(s)

    head_sent[...] = head_kept[...].astype(jnp.bfloat16).reshape(head_sent.shape)
    for step in range(1, cols):
        head_copy(step).start()

    @pl.loop(early, late)
    def _(s):
        send_row(s)

    for step in range(1, cols):
        head_copy(step).wait_recv()
    for part in range(cols):
        span = slice(part * slab_rows, (part + 1) * slab_rows)

        @pl.when(col == part)
        def _():
            head_full[:, span, :] = head_sent[part].astype(f32) * LOG2E

        @pl.when(col != part)
        def _():
            head_full[:, span, :] = head_got[part].astype(f32) * LOG2E

    s_heads = head_full.shape[0]
    usable = lax.broadcasted_iota(jnp.int32, (1, tokens), 1) < length_ref[0]
    head_of_lane = lax.broadcasted_iota(jnp.int32, (1, width), 1) // SINGLE_HEAD_DIM
    blended = jnp.zeros((rows_here, width), f32)
    for head in range(s_heads):
        here = head_of_lane == head
        q_head = jnp.where(here, s_query[...], jnp.zeros_like(s_query[...]))
        scores = lax.dot_general(q_head, s_key[...], NT, preferred_element_type=f32)
        scores = jnp.where(usable, scores + head_full[head], masked_value)
        exponent = jnp.exp2(scores - jnp.max(scores, axis=-1, keepdims=True))
        total = jnp.sum(exponent, axis=-1, keepdims=True)
        weights = (exponent / total).astype(jnp.bfloat16)
        blended = jnp.where(
            here, jnp.dot(weights, s_value[...], preferred_element_type=f32), blended
        )
    s_hidden = (s_gate[...] * blended).astype(jnp.bfloat16)
    share = jnp.dot(s_hidden, single_out_ref[...], preferred_element_type=f32)
    for part in range(cols):
        part_sent[part] = share[:, part * width : (part + 1) * width].astype(jnp.bfloat16)
    for step in range(1, cols):
        part_copy(step).start()

    @pl.loop(late, slab_rows)
    def _(s):
        send_row(s)

    total = rest_ref[...].astype(f32) + part_sent[col].astype(f32)
    for step in range(1, cols):
        part_copy(step).wait_recv()
        total = total + part_got[step].astype(f32)
    single_new_ref[...] = total.astype(jnp.bfloat16)

    for step in range(1, cols):
        col_copy(step).wait_send()
        head_copy(step).wait_send()
        part_copy(step).wait_send()
    for step in range(1, chips):
        chip_copy(step).wait_send()
    for step in range(chips):
        core_copy(step).wait_send()

    @pl.loop(0, slab_rows)
    def _(s):
        own_out(s).wait()
        for step in range(1, cols):
            in_copy(s, step).wait_send()
            out_copy(s, step).wait_send()
            out_copy(s, step).wait_recv()


def per_device(
    pair_rep,
    single_rep,
    length,
    pair_gain,
    pair_proj,
    bias_weight,
    pair_out_weight,
    single_gain,
    single_proj,
    bias_norm_gain,
    single_bias_weight,
    single_out_weight,
):
    rows_here, cols_here, channels = pair_rep.shape
    rows, cols = lax.axis_size("row"), lax.axis_size("col")
    tokens = rows_here * rows
    slab_rows = rows_here // cols
    chips = rows // 2
    heads = bias_weight.shape[1]
    single_heads = single_bias_weight.shape[1]
    heads_here = single_heads // cols
    width = single_proj.shape[2]
    single_proj_t = single_proj.transpose(0, 2, 1)
    bf16, f32 = jnp.bfloat16, jnp.float32
    dma = pltpu.SemaphoreType.DMA
    anywhere = pl.BlockSpec(memory_space=pl.ANY)
    held = pl.BlockSpec(memory_space=pltpu.VMEM)
    pair_out, single_out = pl.pallas_call(
        window_kernel,
        in_specs=[pl.BlockSpec(memory_space=pltpu.SMEM)] + [anywhere] * 6 + [held] * 5,
        out_specs=[anywhere, held],
        out_shape=[
            jax.ShapeDtypeStruct(pair_rep.shape, bf16),
            jax.ShapeDtypeStruct((rows_here, width), bf16),
        ],
        scratch_shapes=[
            pltpu.VMEM(pair_rep.shape, bf16),
            pltpu.VMEM((heads, rows_here, cols_here), f32),
            pltpu.VMEM((heads, rows_here, cols_here), bf16),
            pltpu.VMEM(single_rep.shape, bf16),
            pltpu.VMEM(pair_proj.shape, bf16),
            pltpu.VMEM(pair_out_weight.shape, bf16),
            pltpu.VMEM(single_proj_t.shape, bf16),
            pltpu.VMEM(single_out_weight.shape, bf16),
            pltpu.VMEM((rows_here, width), bf16),
            dma((cols,)),
            dma((5,)),
            pltpu.VMEM((slab_rows, cols, cols_here, channels), bf16),
            pltpu.VMEM((slab_rows, cols, cols_here, channels), bf16),
            pltpu.VMEM((rows, cols, heads, rows_here, cols_here), bf16),
            pltpu.VMEM((heads, tokens, tokens), f32),
            pltpu.VMEM((single_heads, slab_rows, tokens), f32),
            pltpu.VMEM((cols, heads_here, slab_rows, tokens), bf16),
            pltpu.VMEM((cols, heads_here, slab_rows, tokens), bf16),
            pltpu.VMEM((heads_here, rows_here, tokens), f32),
            pltpu.VMEM((rows_here, width), bf16),
            pltpu.VMEM((tokens, width), bf16),
            pltpu.VMEM((tokens, width), bf16),
            pltpu.VMEM((rows_here, width), f32),
            pltpu.VMEM((cols, rows_here, width), bf16),
            pltpu.VMEM((cols, rows_here, width), bf16),
            dma((slab_rows, cols)),
            dma((slab_rows, cols)),
            dma((slab_rows,)),
            dma((slab_rows, cols)),
            dma((slab_rows, cols)),
            dma((slab_rows,)),
            dma((cols,)),
            dma((cols,)),
            dma,
            dma((chips,)),
            dma((chips,)),
            dma((chips,)),
            dma((chips,)),
            dma((cols,)),
            dma((cols,)),
            dma((cols,)),
            dma((cols,)),
        ],
        compiler_params=pltpu.CompilerParams(
            collective_id=0, has_side_effects=True, vmem_limit_bytes=60 * 2**20
        ),
        name="window",
    )(
        length, pair_rep, single_rep, pair_proj, pair_out_weight, single_proj_t, single_out_weight,
        pair_gain, bias_weight.T, bias_norm_gain, single_bias_weight.T, single_gain,
    )
    return (pair_out, single_out)


def solution(mesh):
    in_specs = (
        P("row", "col", None),
        P(),
        P(),
        P(),
        P(),
        P(),
        P(),
        P(),
        P(None, None, "col"),
        P(),
        P(),
        P("col", None),
    )
    out_specs = (P("row", "col", None), P("row", "col"))
    return jax.shard_map(
        per_device, mesh=mesh, in_specs=in_specs, out_specs=out_specs, check_vma=False
    )
```

```python
import math

import jax
import jax.numpy as jnp
from jax import lax
from jax.experimental import pallas as pl
from jax.experimental.pallas import tpu as pltpu
from jax.sharding import PartitionSpec as P

PAIR_HEADS = 8
PAIR_HEAD_DIM = 32
SINGLE_HEAD_DIM = 48
LOG2E = math.log2(math.e)

masked_value = -1e30
NT = (((1,), (1,)), ((), ()))


def normalize(values, scales):
    floated = values.astype(jnp.float32)
    center = jnp.mean(floated, axis=-1, keepdims=True)
    spread = jnp.mean(jnp.square(floated - center), axis=-1, keepdims=True)
    return ((floated - center) * lax.rsqrt(spread + 1e-05) * scales).astype(jnp.bfloat16)


def project(inputs, matrix):
    return jnp.dot(inputs, matrix, preferred_element_type=jnp.float32).astype(jnp.bfloat16)


def project_t(inputs, matrix):
    return lax.dot_general(inputs, matrix, NT, preferred_element_type=jnp.float32).astype(
        jnp.bfloat16
    )


def row_update(rep, gain, proj_ref, out_weight, bias_of):
    channels = rep.shape[1]
    half = channels // 2
    heads_per_half = PAIR_HEADS // 2
    normed = normalize(rep, gain)
    f32 = jnp.float32
    query = jnp.dot(normed, proj_ref[0], preferred_element_type=f32)
    query = (query * (LOG2E / math.sqrt(PAIR_HEAD_DIM))).astype(jnp.bfloat16)
    key = project(normed, proj_ref[1])
    value = project(normed, proj_ref[2])
    gate = jax.nn.sigmoid(jnp.dot(normed, proj_ref[3], preferred_element_type=f32))
    head_of_lane = lax.broadcasted_iota(jnp.int32, (1, half), 1) // PAIR_HEAD_DIM
    halves = []
    for side in range(2):
        span = slice(side * half, (side + 1) * half)
        q_half, k_half, v_half = query[:, span], key[:, span], value[:, span]
        top = bottom = None
        for sub in range(heads_per_half):
            head = side * heads_per_half + sub
            mine = head_of_lane == sub
            q_head = jnp.where(mine, q_half, jnp.zeros_like(q_half))
            scores = lax.dot_general(q_head, k_half, NT, preferred_element_type=f32)
            scores = scores + bias_of(head)
            peak = jnp.max(scores, axis=-1, keepdims=True)
            exponent = jnp.exp2(scores - peak).astype(jnp.bfloat16)
            v_ext = jnp.concatenate([v_half, jnp.ones_like(v_half)], axis=1)
            both = jnp.dot(exponent, v_ext, preferred_element_type=f32)
            num, den = both[:, :half], both[:, half:]
            top = num if top is None else jnp.where(mine, num, top)
            bottom = den if bottom is None else jnp.where(mine, den, bottom)
        halves.append(top / bottom)
    attended = jnp.concatenate(halves, axis=1)
    hidden = (gate * attended).astype(jnp.bfloat16)
    return (
        rep.astype(f32) + jnp.dot(hidden, out_weight, preferred_element_type=f32)
    ).astype(jnp.bfloat16)


def slot(ref, *index):
    return ref.at[index]


def window_kernel(
    length_ref, pair_ref, single_hbm, proj_hbm, out_weight_hbm, single_proj_hbm, single_out_hbm,
    gain_ref, tri_weight_ref, bias_gain_ref, head_weight_ref, single_gain_ref,
    pair_out_ref, single_new_ref,
    local, tri_kept, tri_ref, single_ref, proj_ref, out_weight_ref, single_proj_ref, single_out_ref,
    rest_ref, local_sem, weight_sem,
    slab, fresh, bands, bias_held, head_kept, head_sent, head_got, head_full,
    s_query, s_key, s_value, s_gate, part_sent, part_got,
    in_send, in_recv, in_own, out_send, out_recv, out_own,
    col_send, col_recv, col_own, chip_send, chip_recv, core_send, core_recv,
    head_send, head_recv, part_send, part_recv,
):
    f32 = jnp.float32
    slab_rows, cols, cols_here, channels = slab.shape
    rows, _, heads, rows_here, _ = bands.shape
    tokens = cols * cols_here
    chips = rows // 2
    row, col = lax.axis_index("row"), lax.axis_index("col")
    chip, core = row // 2, lax.rem(row, 2)
    partner = chip * 2 + 1 - core
    mesh_id = pl.DeviceIdType.MESH

    def peer(step):
        return lax.rem(col + step, cols)

    def chip_row(step):
        return lax.rem(chip + step, chips) * 2 + core

    def chip_back(step):
        return lax.rem(chip + chips - step, chips) * 2 + core

    def local_copy(part):
        span = pl.ds(part * slab_rows, slab_rows)
        return pltpu.make_async_copy(pair_ref.at[span], local.at[span], local_sem.at[part])

    weight_copies = [
        pltpu.make_async_copy(src, dst, weight_sem.at[i])
        for i, (src, dst) in enumerate(
            (
                (single_hbm, single_ref),
                (single_proj_hbm, single_proj_ref),
                (proj_hbm, proj_ref),
                (out_weight_hbm, out_weight_ref),
                (single_out_hbm, single_out_ref),
            )
        )
    ]
    for part in range(cols):
        local_copy(part).start()
    for copy in weight_copies:
        copy.start()

    barrier = pltpu.get_barrier_semaphore()
    for step in range(1, cols):
        pl.semaphore_signal(barrier, inc=1, device_id=(row, peer(step)), device_id_type=mesh_id)
    for step in range(1, chips):
        pl.semaphore_signal(barrier, inc=1, device_id=(chip_row(step), col), device_id_type=mesh_id)
    pl.semaphore_signal(barrier, inc=1, device_id=(partner, col), device_id_type=mesh_id)
    pl.semaphore_wait(barrier, cols + chips - 1)

    def remote(src, dst, send, recv, to):
        return pltpu.make_async_remote_copy(
            src_ref=src, dst_ref=dst, send_sem=send, recv_sem=recv,
            device_id=to, device_id_type=mesh_id,
        )

    near = cols // 2
    mirror = peer(near)

    def near_peer(step):
        return col // near * near + lax.rem(lax.rem(col, near) + step, near)

    own_steps = range(1, near)
    mirror_steps = range(near + 1, 2 * near)

    def col_copy(step):
        to = mirror if step == 0 else near_peer(step % near)
        src, place = (tri_ref, col) if step < near else (slot(bands, row, mirror), mirror)
        return remote(
            src, slot(bands, row, place), col_send.at[step], col_recv.at[step], (row, to)
        )

    def chip_copy(step):
        return remote(
            slot(bands, row), slot(bands, row), chip_send.at[step], chip_recv.at[step],
            (chip_row(step), col),
        )

    def core_copy(step):
        band = chip_back(step)
        return remote(
            slot(bands, band), slot(bands, band), core_send.at[step], core_recv.at[step],
            (partner, col),
        )

    def in_copy(s, step):
        to = peer(step)
        return remote(
            slot(pair_ref, to * slab_rows + s), slot(slab, s, col),
            in_send.at[s, step], in_recv.at[s, step], (row, to),
        )

    def own_in(s):
        return pltpu.make_async_copy(
            slot(pair_ref, col * slab_rows + s), slot(slab, s, col), in_own.at[s]
        )

    def out_copy(s, step):
        to = peer(step)
        return remote(
            slot(fresh, s, to), slot(pair_out_ref, col * slab_rows + s),
            out_send.at[s, step], out_recv.at[s, step], (row, to),
        )

    def own_out(s):
        return pltpu.make_async_copy(
            slot(fresh, s, col), slot(pair_out_ref, col * slab_rows + s), out_own.at[s]
        )

    def head_copy(step):
        to = peer(step)
        return remote(
            slot(head_sent, to), slot(head_got, col), head_send.at[step], head_recv.at[step],
            (row, to),
        )

    def part_copy(step):
        to = peer(step)
        return remote(
            slot(part_sent, to), slot(part_got, step), part_send.at[step], part_recv.at[step],
            (row, to),
        )

    def bring_row(s):
        own_in(s).start()
        for step in range(1, cols):
            in_copy(s, step).start()

    bring_row(0)
    group = math.gcd(slab_rows, 6)
    for part in range(cols):
        local_copy(part).wait()

        @pl.loop(0, slab_rows // group)
        def _(i):
            for j in range(group):
                r = part * slab_rows + i * group + j
                tri_kept[:, r, :] = lax.dot_general(
                    tri_weight_ref[...], normalize(local[r], gain_ref[...]), NT,
                    preferred_element_type=f32,
                )

    tri_ref[...] = tri_kept[...].astype(jnp.bfloat16)
    for step in (0, *own_steps):
        col_copy(step).start()
    own_block = pltpu.make_async_copy(tri_ref, slot(bands, row, col), col_own)
    own_block.start()

    ahead = min(3, slab_rows)
    for s in range(1, ahead):
        bring_row(s)
    col_copy(0).wait_recv()
    for step in mirror_steps:
        col_copy(step).start()

    @pl.loop(ahead, slab_rows)
    def _(s):
        bring_row(s)

    for copy in weight_copies:
        copy.wait()

    for step in (*own_steps, *mirror_steps):
        col_copy(step).wait_recv()
    own_block.wait()
    for step in range(1, chips):
        chip_copy(step).start()
    core_copy(0).start()

    s_normed = normalize(single_ref[...], single_gain_ref[...])
    s_key[...] = project_t(s_normed, single_proj_ref[1])
    s_value[...] = project_t(s_normed, single_proj_ref[2])
    width = s_key.shape[1]
    my_rows = pl.ds(pl.multiple_of(row * rows_here, rows_here), rows_here)
    for part in range(cols):

        @pl.when(col == part)
        def _():
            rest_ref[...] = single_ref[my_rows, part * width : (part + 1) * width]

    mine = normalize(
        single_ref[my_rows, :],
        single_gain_ref[...],
    )
    s_query[...] = (
        lax.dot_general(mine, single_proj_ref[0], NT, preferred_element_type=f32)
        * (LOG2E / math.sqrt(SINGLE_HEAD_DIM))
    ).astype(jnp.bfloat16)
    s_gate[...] = jax.nn.sigmoid(
        lax.dot_general(mine, single_proj_ref[3], NT, preferred_element_type=f32)
    )

    def take_band(band):
        start = pl.multiple_of(band * rows_here, rows_here)
        for part in range(cols):
            usable = (
                lax.broadcasted_iota(jnp.int32, (1, 1, cols_here), 2) + part * cols_here
                < length_ref[0]
            )
            piece = bands[band, part].astype(f32) * LOG2E
            bias_held[:, pl.ds(start, rows_here), part * cols_here : (part + 1) * cols_here] = (
                jnp.where(usable, piece, masked_value)
            )

    take_band(row)
    for step in range(1, chips):
        chip_copy(step).wait_recv()
        core_copy(step).start()
        take_band(chip_back(step))
    for step in range(chips):
        core_copy(step).wait_recv()
        take_band(chip_back(step) + 1 - 2 * core)

    early = 2 * slab_rows // 3
    late = slab_rows - slab_rows // 6

    def one_row(s):
        own_in(s).wait()
        for step in range(1, cols):
            in_copy(s, step).wait_recv()
        rep = slab[s].reshape(tokens, channels)
        updated = row_update(
            rep, gain_ref[...], proj_ref, out_weight_ref[...], lambda head: bias_held[head]
        )
        fresh[s] = updated.reshape(cols, cols_here, channels)
        again = normalize(updated, bias_gain_ref[...])
        head_kept[:, s, :] = lax.dot_general(
            head_weight_ref[...], again, NT, preferred_element_type=f32
        )

    def send_row(s):
        own_out(s).start()
        for step in range(1, cols):
            out_copy(s, step).start()

    @pl.loop(0, slab_rows)
    def _(s):
        one_row(s)

        @pl.when(s < early)
        def _():
            send_row(s)

    head_sent[...] = head_kept[...].astype(jnp.bfloat16).reshape(head_sent.shape)
    for step in range(1, cols):
        head_copy(step).start()

    @pl.loop(early, late)
    def _(s):
        send_row(s)

    for step in range(1, cols):
        head_copy(step).wait_recv()
    for part in range(cols):
        span = slice(part * slab_rows, (part + 1) * slab_rows)

        @pl.when(col == part)
        def _():
            head_full[:, span, :] = head_sent[part].astype(f32) * LOG2E

        @pl.when(col != part)
        def _():
            head_full[:, span, :] = head_got[part].astype(f32) * LOG2E

    s_heads = head_full.shape[0]
    usable = lax.broadcasted_iota(jnp.int32, (1, tokens), 1) < length_ref[0]
    head_of_lane = lax.broadcasted_iota(jnp.int32, (1, width), 1) // SINGLE_HEAD_DIM
    blended = jnp.zeros((rows_here, width), f32)
    for head in range(s_heads):
        here = head_of_lane == head
        q_head = jnp.where(here, s_query[...], jnp.zeros_like(s_query[...]))
        scores = lax.dot_general(q_head, s_key[...], NT, preferred_element_type=f32)
        scores = jnp.where(usable, scores + head_full[head], masked_value)
        exponent = jnp.exp2(scores - jnp.max(scores, axis=-1, keepdims=True))
        total = jnp.sum(exponent, axis=-1, keepdims=True)
        weights = (exponent / total).astype(jnp.bfloat16)
        blended = jnp.where(
            here, jnp.dot(weights, s_value[...], preferred_element_type=f32), blended
        )
    s_hidden = (s_gate[...] * blended).astype(jnp.bfloat16)
    share = jnp.dot(s_hidden, single_out_ref[...], preferred_element_type=f32)
    for part in range(cols):
        part_sent[part] = share[:, part * width : (part + 1) * width].astype(jnp.bfloat16)
    for step in range(1, cols):
        part_copy(step).start()

    @pl.loop(late, slab_rows)
    def _(s):
        send_row(s)

    total = rest_ref[...].astype(f32) + part_sent[col].astype(f32)
    for step in range(1, cols):
        part_copy(step).wait_recv()
        total = total + part_got[step].astype(f32)
    single_new_ref[...] = total.astype(jnp.bfloat16)

    for step in range(1, cols):
        head_copy(step).wait_send()
        part_copy(step).wait_send()
    for step in (0, *own_steps, *mirror_steps):
        col_copy(step).wait_send()
    for step in range(1, chips):
        chip_copy(step).wait_send()
    for step in range(chips):
        core_copy(step).wait_send()

    @pl.loop(0, slab_rows)
    def _(s):
        own_out(s).wait()
        for step in range(1, cols):
            in_copy(s, step).wait_send()
            out_copy(s, step).wait_send()
            out_copy(s, step).wait_recv()


def per_device(
    pair_rep,
    single_rep,
    length,
    pair_gain,
    pair_proj,
    bias_weight,
    pair_out_weight,
    single_gain,
    single_proj,
    bias_norm_gain,
    single_bias_weight,
    single_out_weight,
):
    rows_here, cols_here, channels = pair_rep.shape
    rows, cols = lax.axis_size("row"), lax.axis_size("col")
    tokens = rows_here * rows
    slab_rows = rows_here // cols
    chips = rows // 2
    heads = bias_weight.shape[1]
    single_heads = single_bias_weight.shape[1]
    heads_here = single_heads // cols
    width = single_proj.shape[2]
    single_proj_t = single_proj.transpose(0, 2, 1)
    bf16, f32 = jnp.bfloat16, jnp.float32
    dma = pltpu.SemaphoreType.DMA
    anywhere = pl.BlockSpec(memory_space=pl.ANY)
    held = pl.BlockSpec(memory_space=pltpu.VMEM)
    pair_out, single_out = pl.pallas_call(
        window_kernel,
        in_specs=[pl.BlockSpec(memory_space=pltpu.SMEM)] + [anywhere] * 6 + [held] * 5,
        out_specs=[anywhere, held],
        out_shape=[
            jax.ShapeDtypeStruct(pair_rep.shape, bf16),
            jax.ShapeDtypeStruct((rows_here, width), bf16),
        ],
        scratch_shapes=[
            pltpu.VMEM(pair_rep.shape, bf16),
            pltpu.VMEM((heads, rows_here, cols_here), f32),
            pltpu.VMEM((heads, rows_here, cols_here), bf16),
            pltpu.VMEM(single_rep.shape, bf16),
            pltpu.VMEM(pair_proj.shape, bf16),
            pltpu.VMEM(pair_out_weight.shape, bf16),
            pltpu.VMEM(single_proj_t.shape, bf16),
            pltpu.VMEM(single_out_weight.shape, bf16),
            pltpu.VMEM((rows_here, width), bf16),
            dma((cols,)),
            dma((5,)),
            pltpu.VMEM((slab_rows, cols, cols_here, channels), bf16),
            pltpu.VMEM((slab_rows, cols, cols_here, channels), bf16),
            pltpu.VMEM((rows, cols, heads, rows_here, cols_here), bf16),
            pltpu.VMEM((heads, tokens, tokens), f32),
            pltpu.VMEM((single_heads, slab_rows, tokens), f32),
            pltpu.VMEM((cols, heads_here, slab_rows, tokens), bf16),
            pltpu.VMEM((cols, heads_here, slab_rows, tokens), bf16),
            pltpu.VMEM((heads_here, rows_here, tokens), f32),
            pltpu.VMEM((rows_here, width), bf16),
            pltpu.VMEM((tokens, width), bf16),
            pltpu.VMEM((tokens, width), bf16),
            pltpu.VMEM((rows_here, width), f32),
            pltpu.VMEM((cols, rows_here, width), bf16),
            pltpu.VMEM((cols, rows_here, width), bf16),
            dma((slab_rows, cols)),
            dma((slab_rows, cols)),
            dma((slab_rows,)),
            dma((slab_rows, cols)),
            dma((slab_rows, cols)),
            dma((slab_rows,)),
            dma((cols,)),
            dma((cols,)),
            dma,
            dma((chips,)),
            dma((chips,)),
            dma((chips,)),
            dma((chips,)),
            dma((cols,)),
            dma((cols,)),
            dma((cols,)),
            dma((cols,)),
        ],
        compiler_params=pltpu.CompilerParams(
            collective_id=0, has_side_effects=True, vmem_limit_bytes=60 * 2**20
        ),
        name="window",
    )(
        length, pair_rep, single_rep, pair_proj, pair_out_weight, single_proj_t, single_out_weight,
        pair_gain, bias_weight.T, bias_norm_gain, single_bias_weight.T, single_gain,
    )
    return (pair_out, single_out)


def solution(mesh):
    in_specs = (
        P("row", "col", None),
        P(),
        P(),
        P(),
        P(),
        P(),
        P(),
        P(),
        P(None, None, "col"),
        P(),
        P(),
        P("col", None),
    )
    out_specs = (P("row", "col", None), P("row", "col"))
    return jax.shard_map(
        per_device, mesh=mesh, in_specs=in_specs, out_specs=out_specs, check_vma=False
    )
```
